512 devices in a mesh: leaf: 32 (over y, x, core), grp: 16 (over z).
Axes of the slice: x: 4, y: 4, z: 16, core: 2. Of those that a mesh axis runs over, the one named last changes fastest.
Arguments:
- rhs_local: float32 [32, 4, 1024, 128], P('leaf', None, 'grp'), may hold values from -6 to 6
- diag_inv_local: float32 [32, 4, 1024, 1024], P('leaf', None, 'grp'), may hold values from -0.1875 to 0.1875
- sub_local: float32 [32, 3, 1024, 1024], P('leaf', None, 'grp'), may hold values from -0.1875 to 0.1875
- tiles: float32 [32, 16, 3, 128, 1024], P('leaf', 'grp'), may hold values from -0.046875 to 0.046875
- tile_block: int32 [32, 16, 3], P('leaf', 'grp'), may hold values from 0 to 15
- tile_source: int32 [32, 16, 3], P('leaf', 'grp'), may hold values from 0 to 3
- tile_count: int32 [32, 16], P('leaf', 'grp'), may hold values from 1 to 3, as said below
- rhs_anc: float32 [2, 1024, 128], P(None, 'grp', 'leaf'), may hold values from -6 to 6
- diag_inv_anc: float32 [2, 1024, 1024], P(None, 'grp'), may hold values from -0.1875 to 0.1875
- sub_anc: float32 [1, 1024, 1024], P(None, 'grp'), may hold values from -0.1875 to 0.1875
Outputs:
- solution_local: float32 [32, 4, 1024, 128], P('leaf', None, 'grp')
- solution_anc: float32 [2, 1024, 128], P(None, 'grp', 'leaf')
The draws below stay inside these ranges and needn't reach their ends.
Inputs may be any that keep to these rules, and one draw needn't show every extreme that they name: `tile_count`: some device holds exactly 3 live tiles.
All inputs are finite; a program needn't handle non-finite values.
Results may differ from the reference program's by a relative error of at most 0.0003.
Values sent between devices are 32-bit elements; how exact they have to be, the bound alone decides.
A program may use at most 64 MiB of HBM per device.

```python
import math
import jax
import jax.numpy as jnp
import numpy as np
from jax import lax

NS = 1024
RHS = 128
TILE = 128
CHAIN = 4
ANC = 2
MAXT = 3
GROUPS = 32
MEMBERS = 16
BLOCKS = 16


def draw_tile_count(key, part):
    first, second = jax.random.split(key)
    total = GROUPS * MEMBERS
    heavy = jax.random.randint(first, (total,), 0, 4) == 3
    counts = jnp.where(heavy, MAXT, 1)
    forced = jax.random.randint(second, (), 0, total)
    counts = jnp.where(jnp.arange(total, dtype=jnp.int32) == forced, MAXT, counts)
    return counts.reshape(GROUPS, MEMBERS).astype(jnp.int32)


def set_ends(result, rng, low, high):
    shape = result.shape
    index_at = [jax.random.randint(jax.random.fold_in(rng, axis), (), 0, shape[axis]) for axis in range(len(shape))]
    result = result.at[tuple(index_at)].set(low)
    longest = shape.index(max(shape))
    index_at[longest] = (index_at[longest] + 1) % shape[longest]
    return result.at[tuple(index_at)].set(high)


def block_levels(stream_key, shape, pieces, smallest, top_value):
    loudness = 1.0
    for dim, shards_of in pieces:
        heights = jax.random.uniform(jax.random.fold_in(jax.random.fold_in(stream_key, 6), dim), (shards_of,), jnp.float32, smallest / len(pieces), top_value / len(pieces))
        loudness = loudness * jnp.repeat(jnp.exp(heights), shape[dim] // shards_of).reshape((-1,) + (1,) * (len(shape) - 1 - dim))
    return loudness


def rank_table(number_of, skew):
    loads = [(1 << 20) // math.isqrt(rank ** skew) + 1 for rank in range(1, number_of + 1)]
    width = 1 + sum(loads) // (1 << 30)
    return np.cumsum(np.array([max(1, weight // width) for weight in loads]))


def skewed_ids(key, dims, number_of, skew):
    table = rank_table(number_of, skew)
    lot = jax.random.randint(jax.random.fold_in(key, 1), dims, 0, int(table[number_of - 1]))
    rank = jnp.searchsorted(jnp.asarray(table, jnp.int32), lot, side="right")
    return jax.random.permutation(jax.random.fold_in(key, 2), number_of)[rank].astype(jnp.int32)


def normal_values(own_key, shape, spread, reach, pieces=(), kind=jnp.bfloat16):
    factor_of = block_levels(own_key, shape, pieces, -0.22, 0.18) if pieces else 1.0
    entries = jax.random.normal(own_key, shape, jnp.float32) * spread * factor_of
    return jnp.minimum(jnp.maximum(entries, -reach), reach).astype(kind)


def setup_inputs(seed: int = 0) -> dict:
    arg_keys = jax.random.split(jax.random.key(seed), 11)
    return {
        "rhs_local": normal_values(arg_keys[0], (GROUPS, CHAIN, NS, RHS), 1.0, 6.0, ((0, 32), (2, 16)), jnp.float32),
        "diag_inv_local": normal_values(arg_keys[1], (GROUPS, CHAIN, NS, NS), NS ** -0.5, 0.1875, ((0, 32), (2, 16)), jnp.float32),
        "sub_local": normal_values(arg_keys[2], (GROUPS, CHAIN - 1, NS, NS), NS ** -0.5, 0.1875, ((0, 32), (2, 16)), jnp.float32),
        "tiles": normal_values(arg_keys[3], (GROUPS, MEMBERS, MAXT, TILE, NS), (NS * 16) ** -0.5, 0.046875, ((0, 32), (1, 16)), jnp.float32),
        "tile_block": set_ends(skewed_ids(arg_keys[4], (GROUPS, MEMBERS, MAXT), BLOCKS, 2), jax.random.fold_in(arg_keys[4], 3), 0, BLOCKS - 1).astype(jnp.int32),
        "tile_source": set_ends(jax.random.randint(arg_keys[5], (GROUPS, MEMBERS, MAXT), 0, CHAIN), jax.random.fold_in(arg_keys[5], 1), 0, CHAIN - 1).astype(jnp.int32),
        "tile_count": draw_tile_count(jax.random.fold_in(arg_keys[10], 71), 0),
        "rhs_anc": normal_values(arg_keys[7], (ANC, NS, RHS), 1.0, 6.0, ((1, 16), (2, 32)), jnp.float32),
        "diag_inv_anc": normal_values(arg_keys[8], (ANC, NS, NS), NS ** -0.5, 0.1875, ((1, 16),), jnp.float32),
        "sub_anc": normal_values(arg_keys[9], (ANC - 1, NS, NS), NS ** -0.5, 0.1875, ((1, 16),), jnp.float32),
    }


highest = lax.Precision.HIGHEST


def product(left, right):
    return jnp.dot(left, right, precision=highest, preferred_element_type=jnp.float32)


def reference(rhs_local, diag_inv_local, sub_local, tiles, tile_block, tile_source, tile_count, rhs_anc, diag_inv_anc, sub_anc):
    def solve_group(inputs):
        rhs_group, inverse_group, below_group = inputs
        solved = []
        update = jnp.zeros_like(rhs_group[0])
        for current in range(CHAIN):
            residual = rhs_group[current] - update
            solution = product(inverse_group[current], residual)
            solved.append(solution)
            if current + 1 < CHAIN:
                update = product(below_group[current], solution)
        return jnp.stack(solved)

    solution_local = lax.map(solve_group, (rhs_local, diag_inv_local, sub_local))

    def add_group(running, inputs):
        tiles_group, block_group, source_group, count_group, solved_group = inputs
        chosen = solved_group[source_group]
        tile_terms = jnp.einsum("gmtk,gmkr->gmtr", tiles_group, chosen, precision=highest, preferred_element_type=jnp.float32)
        active = (jnp.arange(MAXT, dtype=jnp.int32)[None, :] < count_group[:, None]).astype(jnp.float32)
        onehot = (block_group[:, :, None] == jnp.arange(BLOCKS, dtype=jnp.int32)[None, None, :]).astype(jnp.float32)
        onehot = onehot * active[:, :, None]
        added = jnp.einsum("gmb,gmtr->btr", onehot, tile_terms, precision=highest, preferred_element_type=jnp.float32)
        return running + added, None

    initial = jnp.zeros((BLOCKS, TILE, RHS), jnp.float32)
    summed, unused = lax.scan(add_group, initial, (tiles, tile_block, tile_source, tile_count, solution_local))
    partial_value = summed.reshape(ANC, NS, RHS)
    ancestors_solved = []
    update = jnp.zeros_like(rhs_anc[0])
    for ancestor in range(ANC):
        residual = rhs_anc[ancestor] - partial_value[ancestor] - update
        solution = product(diag_inv_anc[ancestor], residual)
        ancestors_solved.append(solution)
        if ancestor + 1 < ANC:
            update = product(sub_anc[ancestor], solution)
    return solution_local, jnp.stack(ancestors_solved)
```

```python
import jax
import jax.numpy as jnp
from jax import lax
from jax.experimental import pallas as pl
from jax.experimental.pallas import tpu as pltpu
from jax.sharding import PartitionSpec as P

HI = lax.Precision.HIGHEST
F32 = jnp.float32
N = 16
SIDE = 4
CHAIN = 4
ROWS = 64
RHS = 128
TILES = 3
SLOTS = 9

CHILDREN = {0: (3, 1), 3: (6, 4, 2), 6: (8, 7, 5)}
ORDER = (1, 3, 2, 4, 6, 5, 7, 8)
EDGES = sorted({abs(b - a) for a, bs in CHILDREN.items() for b in bs})


def dot(a, b):
    return jnp.dot(a, b, precision=HI, preferred_element_type=F32)


def dot_nt(a, b):
    return lax.dot_general(a, b, (((1,), (1,)), ((), ())), precision=HI, preferred_element_type=F32)


def kernel(
    block_s, source_s, count_s, rhs, rhs_anc, dinv_h, sub_h, tiles_h, dinva_h, suba_h,
    out_local, out_anc,
    dinv, sub, tiles, dinva, suba,
    pd, pt, gr, gx, gl, gz, old, cells, pool, theirs, inbox1, mid, inbox2, zbuf, ebuf, fbuf, relmat, give, take, prow,
    load_sem, send_sem, recv_sem, pair_send, pair_recv, one_send, one_recv, two_send, two_recv,
    e_send, e_recv, f_send, f_recv, last_send, last_recv,
):
    me = lax.axis_index("grp")
    leaf = lax.axis_index("leaf")
    core = lax.rem(leaf, 2)
    x = lax.rem(lax.div(leaf, 2), SIDE)
    y = lax.div(leaf, 2 * SIDE)
    partner = leaf + 1 - 2 * core
    p_one = jnp.where(core == 0, x, y)
    p_two = jnp.where(core == 0, y, x)

    def leaf_of(one, two):
        xx = jnp.where(core == 0, one, two)
        yy = jnp.where(core == 0, two, one)
        return (yy * SIDE + xx) * 2 + core

    def z_at(step):
        return lax.rem(me + (step + 2 * N), N)

    one_of = [leaf_of(lax.rem(p_one + d, SIDE), p_two) for d in range(SIDE)]
    two_of = [leaf_of(p_one, lax.rem(p_two + d, SIDE)) for d in range(SIDE)]

    loads = [
        pltpu.make_async_copy(src, dst, load_sem.at[i])
        for i, (src, dst) in enumerate(
            ((dinv_h.at[0], dinv), (sub_h.at[0], sub), (tiles_h.at[0, 0], tiles), (dinva_h, dinva), (suba_h, suba))
        )
    ]
    for load in loads:
        load.start()

    prow[...] = jnp.zeros_like(prow)
    ebuf[0] = jnp.zeros((8, 128), F32)
    give[2] = jnp.zeros((8, 128), F32)
    take[0] = jnp.zeros((8, 128), F32)
    barrier = pltpu.get_barrier_semaphore()
    greeted = 0
    for step in EDGES:
        for sign in (1, -1):
            pl.semaphore_signal(barrier, inc=1, device_id={"grp": z_at(sign * step)}, device_id_type=pl.DeviceIdType.MESH)
            greeted += 1
    for other in (partner, *one_of[1:], *two_of[1:]):
        pl.semaphore_signal(barrier, inc=1, device_id={"leaf": other}, device_id_type=pl.DeviceIdType.MESH)
        greeted += 1
    pl.semaphore_wait(barrier, greeted)

    def buffer(k):
        if k == 8:
            return gz
        if k == 7:
            return gl
        return gr.at[k // 2] if k % 2 == 0 else gx.at[k // 2]

    def view(k, d, b):
        buf = buffer(k)
        if b == 0:
            return rhs.at[0, 0] if k == 0 else buf.at[0, 0:ROWS]
        if b == 8:
            return buf.at[0, ROWS + 32 * d : ROWS + 32 * d + 32]
        return buf.at[b, ROWS * d : ROWS * d + ROWS]

    def edge(k, d, a, b):
        src = view(k, d, a)
        if b == 8:
            src = src.at[32 * d : 32 * d + 32]
        step = b - a if d == 0 else a - b
        return pltpu.make_async_remote_copy(
            src_ref=src,
            dst_ref=view(k, d, b),
            send_sem=send_sem.at[k, d, b - 1],
            recv_sem=recv_sem.at[k, d, b - 1],
            device_id={"grp": z_at(step)},
            device_id_type=pl.DeviceIdType.MESH,
        )

    parent = {b: a for a, bs in CHILDREN.items() for b in bs}

    def gather(k, consume, between=None):
        for b in CHILDREN[0]:
            for d in (0, 1):
                edge(k, d, 0, b).start()
        if between is not None:
            between(0)
        consume(0)
        for place, b in enumerate(ORDER):
            for d in (0, 1):
                edge(k, d, parent[b], b).wait_recv()
                for c in CHILDREN.get(b, ()):
                    edge(k, d, b, c).start()
            consume(b)
            if between is not None:
                between(place + 1)

    def finish(k):
        for b in range(1, 9):
            for d in (0, 1):
                edge(k, d, parent[b], b).wait_send()

    shift = lax.rem((N - me) * ROWS, N * ROWS)

    def turned(matrix):
        return pltpu.roll(matrix, shift, axis=1)

    def paired(matrix, j):
        if j == 0:
            return matrix[:, 0:ROWS]
        if j == 8:
            return matrix[:, 8 * ROWS : 9 * ROWS]
        return jnp.concatenate(
            [matrix[:, (N - j) * ROWS : (N - j + 1) * ROWS], matrix[:, j * ROWS : (j + 1) * ROWS]], axis=1
        )

    def prepare(i):
        matrix = turned(dinv[i // 2] if i % 2 == 0 else sub[i // 2])
        for j in range(SLOTS):
            piece = paired(matrix, j)
            pd[i, j, :, 0 : piece.shape[1]] = piece

    def prepare_tile(m):
        matrix = turned(tiles[m])
        for j in range(SLOTS):
            piece = paired(matrix, j)
            pt[j, m * 128 : (m + 1) * 128, 0 : piece.shape[1]] = piece

    def chunk(buf, j):
        if j == 0:
            return buf[0, 0:ROWS]
        if j == 8:
            return buf[0, ROWS : 2 * ROWS]
        return buf[j]

    def multiply(i, k):
        total = []
        buf = buffer(k)

        def consume(b):
            left = pd[i, b, :, 0:ROWS] if b in (0, 8) else pd[i, b]
            right = rhs[0, 0] if (k == 0 and b == 0) else chunk(buf, b)
            term = dot(left, right)
            if total:
                total[0] = total[0] + term
            else:
                total.append(term)

        return total, consume

    sources = [source_s[0, 0, m] for m in range(TILES)]
    blocks = [block_s[0, 0, m] for m in range(TILES)]
    live = count_s[0, 0]

    def earlier(b):
        for m in range(TILES):
            rows = slice(m * 128, (m + 1) * 128)
            left = pt[b, rows, 0:ROWS] if b in (0, 8) else pt[b, rows]
            at = jnp.minimum(sources[m], CHAIN - 2)
            if b == 0:
                right = gx[at, 0, 0:ROWS]
            elif b == 8:
                right = gx[at, 0, ROWS : 2 * ROWS]
            else:
                right = gx[at, b]
            term = dot(left, right)
            if b == 0:
                old[m] = term
            else:
                old[m] += term

    loads[0].wait()
    loads[1].wait()
    for s in range(CHAIN):
        k = 2 * s
        total, consume = multiply(k, k)
        if s == 0:

            def between(step):
                if step == 0:
                    prepare(0)
                elif step < 7:
                    prepare(step)

        elif s == 1:

            def between(step):
                if step == 0:
                    loads[2].wait()
                    loads[3].wait()
                    loads[4].wait()
                elif step <= TILES:
                    prepare_tile(step - 1)
                elif step == 4:
                    relmat[0] = turned(suba[0])
                elif step == 5:
                    relmat[1] = turned(dinva[1])

        elif s == 2:
            between = None
        else:

            def between(step):
                earlier(0 if step == 0 else ORDER[step - 1])

        gather(k, consume, between)
        solved = total[0]
        buffer(k + 1)[0, 0:ROWS] = solved
        out_local[0, s] = solved
        if s + 1 < CHAIN:
            total, consume = multiply(k + 1, k + 1)
            gather(k + 1, consume)
            buffer(k + 2)[0, 0:ROWS] = rhs[0, s + 1] - total[0]
    for m in range(TILES):
        old[m] = jnp.where(sources[m] == CHAIN - 1, 0.0, old[m])

    last = []

    def consume_last(b):
        left = pt[b, :, 0:ROWS] if b in (0, 8) else pt[b]
        term = dot(left, chunk(gl, b))
        if last:
            last[0] = last[0] + term
        else:
            last.append(term)

    gather(7, consume_last)
    for m in range(TILES):
        term = jnp.where(sources[m] == CHAIN - 1, last[0][m * 128 : (m + 1) * 128], old[m])
        term = jnp.where(m < live, term, 0.0)
        cells[m] = jnp.transpose(term).reshape(N, 8, 128)

    half = lax.rem(me, 2)
    home = lax.div(me, 2)
    lane = lax.broadcasted_iota(jnp.int32, (8, 128), 1)
    sub_at = lax.broadcasted_iota(jnp.int32, (8, 128), 0)
    inside = jnp.logical_and(lax.div(lane, ROWS) == half, lax.div(sub_at, 4) == core)
    for a in range(2):
        prow[0:ROWS, 0:4] = rhs_anc[a]
        tall = jnp.transpose(prow[...])
        quad = tall[0:8]
        wide = jnp.where(sub_at < 4, quad, pltpu.roll(quad, 4, axis=0))
        wide = jnp.where(lane < ROWS, wide, pltpu.roll(wide, ROWS, axis=1))
        give[a] = jnp.where(inside, wide, 0.0)

    def build(role, out):
        for d in range(SIDE):
            for e in range(SIDE):
                xx = jnp.where(role == 0, lax.rem(x + d, SIDE), lax.rem(x + e, SIDE))
                yy = jnp.where(role == 0, lax.rem(y + e, SIDE), lax.rem(y + d, SIDE))
                cell = yy * SIDE + xx
                pieces = [cells[m, cell] for m in range(TILES)]
                for b in range(8):
                    value = jnp.zeros((8, 128), F32)
                    for m in range(TILES):
                        value = value - jnp.where(blocks[m] == role * 8 + b, pieces[m], 0.0)
                    if d == 0 and e == 0:
                        value = value + jnp.where(home == b, give[role], 0.0)
                    out[d, e, b] = value

    def remote(src, dst, send, recv, **where):
        return pltpu.make_async_remote_copy(
            src_ref=src, dst_ref=dst, send_sem=send, recv_sem=recv, device_id=where, device_id_type=pl.DeviceIdType.MESH
        )

    build(1 - core, theirs)
    pairs = [remote(theirs.at[d], pool.at[d], pair_send.at[d], pair_recv.at[d], leaf=partner) for d in range(SIDE)]
    for d in (2, 1, 3, 0):
        pairs[d].start()
    build(core, mid)
    ones = [None] + [
        remote(mid.at[d], inbox1.at[d - 1], one_send.at[d - 1], one_recv.at[d - 1], leaf=one_of[d]) for d in range(1, SIDE)
    ]
    for d in (2, 1, 3, 0):
        pairs[d].wait_recv()
        mid[d] = mid[d] + pool[d]
        if d:
            ones[d].start()
    for d in (1, 3, 2):
        ones[d].wait_recv()
    zbuf[...] = mid[0] + inbox1[0] + inbox1[1] + inbox1[2]
    twos = [None] + [
        remote(zbuf.at[d], inbox2.at[d - 1], two_send.at[d - 1], two_recv.at[d - 1], leaf=two_of[d]) for d in range(1, SIDE)
    ]
    for d in (2, 1, 3):
        twos[d].start()
    for d in (1, 3, 2):
        twos[d].wait_recv()
    gz[0, 0:ROWS] = (zbuf[0] + inbox2[0] + inbox2[1] + inbox2[2]).reshape(ROWS, RHS)

    sums = []

    def add_up(b):
        piece = chunk(gz, b)
        if b not in (0, 8):
            piece = piece[0:ROWS] + piece[ROWS : 2 * ROWS]
        if sums:
            sums[0] = sums[0] + piece
        else:
            sums.append(piece)

    gather(8, add_up)
    wanted = sums[0]
    first = jnp.zeros((8, ROWS), F32)
    for b in range(8):
        first = first + dot_nt(wanted[b * 8 : b * 8 + 8], dinva[core, :, b * 128 : (b + 1) * 128])

    def row_of(buf):
        return jnp.concatenate([buf[(N - r) % N, :, 0:ROWS] for r in range(N)], axis=1)

    ebuf[0, :, 0:ROWS] = first

    def e_copy(t):
        return remote(ebuf.at[0], ebuf.at[t], e_send.at[t], e_recv.at[t], grp=z_at(t))

    def f_copy(t):
        there = {"leaf": partner} if t == 0 else {"leaf": partner, "grp": z_at(t)}
        return remote(give.at[2], fbuf.at[t], f_send.at[t], f_recv.at[t], **there)

    def swap():
        return remote(take.at[0], take.at[1], last_send.at[0], last_recv.at[0], leaf=partner)

    order = sorted(range(1, N), key=lambda t: -min(t, N - t))

    @pl.when(core == 0)
    def _():
        for t in order:
            e_copy(t).start()
        take[0, :, 0:ROWS] = ebuf[0, :, 0:ROWS]
        swap().start()
        for t in reversed(order):
            e_copy(t).wait_recv()
        give[2, :, 0:ROWS] = dot_nt(row_of(ebuf), relmat[0])
        for t in order:
            f_copy(t).start()
        f_copy(0).start()
        for t in range(N):
            f_copy(t).wait_send()
        for t in order:
            e_copy(t).wait_send()

    @pl.when(core == 1)
    def _():
        for t in [0, *reversed(order)]:
            f_copy(t).wait_recv()
        take[0, :, 0:ROWS] = ebuf[0, :, 0:ROWS] - dot_nt(row_of(fbuf), relmat[1])
        swap().start()

    swap().wait_recv()
    for a in range(2):
        kept = jnp.where(core == a, take[0], take[1])
        kept = jnp.where(core == 0, kept, pltpu.roll(kept, 4, axis=0))
        prow[0:8, :] = kept
        tall = jnp.transpose(prow[...])
        out_anc[a] = tall[0:ROWS, 0:4]

    swap().wait_send()
    for k in range(9):
        finish(k)
    for d in range(SIDE):
        pairs[d].wait_send()
        if d:
            ones[d].wait_send()
            twos[d].wait_send()


def on_device(rhs_local, diag_inv_local, sub_local, tiles, tile_block, tile_source, tile_count, rhs_anc, diag_inv_anc, sub_anc):
    vmem = pl.BlockSpec(memory_space=pltpu.VMEM)
    smem = pl.BlockSpec(memory_space=pltpu.SMEM)
    hbm = pl.BlockSpec(memory_space=pl.ANY)
    dma = pltpu.SemaphoreType.DMA
    return pl.pallas_call(
        kernel,
        out_shape=(
            jax.ShapeDtypeStruct((1, CHAIN, ROWS, RHS), F32),
            jax.ShapeDtypeStruct((2, ROWS, 4), F32),
        ),
        in_specs=[smem, smem, smem, vmem, vmem, hbm, hbm, hbm, hbm, hbm],
        out_specs=(vmem, vmem),
        scratch_shapes=[
            pltpu.VMEM((4, ROWS, 1024), F32),
            pltpu.VMEM((3, ROWS, 1024), F32),
            pltpu.VMEM((TILES, 128, 1024), F32),
            pltpu.VMEM((2, ROWS, 1024), F32),
            pltpu.VMEM((1, ROWS, 1024), F32),
            pltpu.VMEM((7, SLOTS, ROWS, 128), F32),
            pltpu.VMEM((SLOTS, TILES * 128, 128), F32),
            pltpu.VMEM((4, 8, 128, RHS), F32),
            pltpu.VMEM((3, 8, 128, RHS), F32),
            pltpu.VMEM((8, 128, RHS), F32),
            pltpu.VMEM((8, 128, RHS), F32),
            pltpu.VMEM((TILES, 128, RHS), F32),
            pltpu.VMEM((TILES, N, 8, 128), F32),
            pltpu.VMEM((SIDE, SIDE, 8, 8, 128), F32),
            pltpu.VMEM((SIDE, SIDE, 8, 8, 128), F32),
            pltpu.VMEM((3, SIDE, 8, 8, 128), F32),
            pltpu.VMEM((SIDE, SIDE, 8, 8, 128), F32),
            pltpu.VMEM((3, 8, 8, 128), F32),
            pltpu.VMEM((SIDE, 8, 8, 128), F32),
            pltpu.VMEM((N, 8, 128), F32),
            pltpu.VMEM((N, 8, 128), F32),
            pltpu.VMEM((2, ROWS, 1024), F32),
            pltpu.VMEM((3, 8, 128), F32),
            pltpu.VMEM((2, 8, 128), F32),
            pltpu.VMEM((128, 128), F32),
            dma((5,)),
            dma((9, 2, 8)),
            dma((9, 2, 8)),
            dma((SIDE,)),
            dma((SIDE,)),
            dma((3,)),
            dma((3,)),
            dma((3,)),
            dma((3,)),
            dma((N,)),
            dma((N,)),
            dma((N,)),
            dma((N,)),
            dma((1,)),
            dma((1,)),
        ],
        compiler_params=pltpu.CompilerParams(
            collective_id=0, has_side_effects=True, vmem_limit_bytes=56 * 1024 * 1024
        ),
    )(tile_block, tile_source, tile_count, rhs_local, rhs_anc, diag_inv_local, sub_local, tiles, diag_inv_anc, sub_anc)


def solution(mesh):
    return jax.shard_map(
        on_device,
        mesh=mesh,
        in_specs=(
            P("leaf", None, "grp", None),
            P("leaf", None, "grp", None),
            P("leaf", None, "grp", None),
            P("leaf", "grp", None, None, None),
            P("leaf", "grp", None),
            P("leaf", "grp", None),
            P("leaf", "grp"),
            P(None, "grp", "leaf"),
            P(None, "grp", None),
            P(None, "grp", None),
        ),
        out_specs=(P("leaf", None, "grp", None), P(None, "grp", "leaf")),
        check_vma=False,
    )
```

```python
import jax
import jax.numpy as jnp
from jax import lax
from jax.experimental import pallas as pl
from jax.experimental.pallas import tpu as pltpu
from jax.sharding import PartitionSpec as P

HI = lax.Precision.HIGHEST
F32 = jnp.float32
N = 16
SIDE = 4
CHAIN = 4
ROWS = 64
RHS = 128
TILES = 3
SLOTS = 9

CHILDREN = {0: (5, 2, 1), 2: (3,), 5: (8, 7, 6, 4)}
RELAYS = ((5, 2),)
EARLY = (1, 2, 5)
LATE = (3, 6, 4, 7, 8)
RING = {i: (i + 1,) for i in range(8)}
PIECES = 2
EDGES = sorted({abs(b - a) for tree in (CHILDREN, RING) for a, bs in tree.items() for b in bs})


def dot(a, b):
    return jnp.dot(a, b, precision=HI, preferred_element_type=F32)


def dot_nt(a, b):
    return lax.dot_general(a, b, (((1,), (1,)), ((), ())), precision=HI, preferred_element_type=F32)


def kernel(
    block_s, source_s, count_s, rhs, rhs_anc, dinv_h, sub_h, tiles_h, dinva_h, suba_h,
    out_local, out_anc,
    dinv, sub, tiles, dinva, suba,
    pd, pt, gr, gx, gl, gz, old, cells, pool, theirs, inbox1, mid, inbox2, zbuf, gb, tacc, tfull, wfull, give, swap_out, swap_in, prow,
    load_sem, send_sem, recv_sem, pair_send, pair_recv, one_send, one_recv, two_send, two_recv,
    t_send, t_recv, w_send, w_recv, swap_send, swap_recv,
):
    me = lax.axis_index("grp")
    leaf = lax.axis_index("leaf")
    core = lax.rem(leaf, 2)
    x = lax.rem(lax.div(leaf, 2), SIDE)
    y = lax.div(leaf, 2 * SIDE)
    partner = leaf + 1 - 2 * core
    p_one = jnp.where(core == 0, x, y)
    p_two = jnp.where(core == 0, y, x)

    def leaf_of(one, two):
        xx = jnp.where(core == 0, one, two)
        yy = jnp.where(core == 0, two, one)
        return (yy * SIDE + xx) * 2 + core

    def z_at(step):
        return lax.rem(me + (step + 2 * N), N)

    one_of = [leaf_of(lax.rem(p_one + d, SIDE), p_two) for d in range(SIDE)]
    two_of = [leaf_of(p_one, lax.rem(p_two + d, SIDE)) for d in range(SIDE)]

    loads = [
        pltpu.make_async_copy(src, dst, load_sem.at[i])
        for i, (src, dst) in enumerate(
            ((dinv_h.at[0], dinv), (sub_h.at[0], sub), (tiles_h.at[0, 0], tiles), (dinva_h, dinva), (suba_h, suba))
        )
    ]
    for load in loads:
        load.start()

    prow[...] = jnp.zeros_like(prow)
    swap_out[...] = jnp.zeros_like(swap_out)
    barrier = pltpu.get_barrier_semaphore()
    greeted = 0
    for step in EDGES:
        for sign in (1, -1):
            pl.semaphore_signal(barrier, inc=1, device_id={"grp": z_at(sign * step)}, device_id_type=pl.DeviceIdType.MESH)
            greeted += 1
    near = [((lax.div(y, 2) * 2 + dy) * SIDE + dx) * 2 + 1 - core for dy in range(2) for dx in range(SIDE)]
    for other in (*near, *one_of[1:], *two_of[1:]):
        pl.semaphore_signal(barrier, inc=1, device_id={"leaf": other}, device_id_type=pl.DeviceIdType.MESH)
        greeted += 1
    pl.semaphore_wait(barrier, greeted)

    def buffer(k):
        if k == 9:
            return gb
        if k == 8:
            return gz
        if k == 7:
            return gl
        return gr.at[k // 2] if k % 2 == 0 else gx.at[k // 2]

    part = ROWS // PIECES

    def view(k, d, b, p):
        buf = buffer(k)
        if b == 0:
            return rhs.at[0, 0, p * part : (p + 1) * part] if k == 0 else buf.at[0, p * part : (p + 1) * part]
        base = ROWS if b == 8 else ROWS * d
        return buf.at[b % 8, base + p * part : base + (p + 1) * part]

    def ways(b, p):
        return (0, 1) if b < 8 else (2 * p // PIECES,)

    def edge(k, d, a, b, p):
        step = b - a if d == 0 else a - b
        return pltpu.make_async_remote_copy(
            src_ref=view(k, d, a, p),
            dst_ref=view(k, d, b, p),
            send_sem=send_sem.at[k, d, b - 1, p],
            recv_sem=recv_sem.at[k, d, b - 1, p],
            device_id={"grp": z_at(step)},
            device_id_type=pl.DeviceIdType.MESH,
        )

    def tree(k):
        return RING if k == 9 else CHILDREN

    parents = {k: {b: a for a, bs in tree(k).items() for b in bs} for k in range(10)}

    def send_own(k):
        for b in tree(k)[0]:
            for p in range(PIECES):
                for d in ways(b, p):
                    edge(k, d, 0, b, p).start()

    def receive(k, b):
        for p in range(PIECES):
            for d in ways(b, p):
                edge(k, d, parents[k][b], b, p).wait_recv()

    def pass_on(k, relays):
        for p in range(PIECES):
            for b in relays:
                for d in ways(b, p):
                    edge(k, d, parents[k][b], b, p).wait_recv()
                for c in tree(k)[b]:
                    for d in ways(c, p):
                        edge(k, d, b, c, p).start()

    def gather(k, consume, first=None, second=None):
        send_own(k)
        if first is not None:
            first()
        consume(0)
        relays = [b for phase in RELAYS for b in phase]
        pass_on(k, RELAYS[0])
        for b in EARLY:
            if b not in relays:
                receive(k, b)
            consume(b)
        for phase in RELAYS[1:]:
            pass_on(k, phase)
            for b in phase:
                consume(b)
        if second is not None:
            second()
        for b in LATE:
            receive(k, b)
            consume(b)

    def finish(k):
        for b, a in parents[k].items():
            for p in range(PIECES):
                for d in ways(b, p):
                    edge(k, d, a, b, p).wait_send()

    shift = lax.rem((N - me) * ROWS, N * ROWS)

    def turned(matrix):
        return pltpu.roll(matrix, shift, axis=1)

    def paired(matrix, j):
        if j == 0:
            return matrix[:, 0:ROWS]
        if j == 8:
            return matrix[:, 8 * ROWS : 9 * ROWS]
        return jnp.concatenate(
            [matrix[:, (N - j) * ROWS : (N - j + 1) * ROWS], matrix[:, j * ROWS : (j + 1) * ROWS]], axis=1
        )

    def store_pairs(i, matrix):
        for j in range(SLOTS):
            piece = paired(matrix, j)
            pd[i, j, :, 0 : piece.shape[1]] = piece

    def prepare(*which):
        for i in which:
            store_pairs(i, turned(dinv[i // 2] if i % 2 == 0 else sub[i // 2]))

    def prepare_tile(m):
        matrix = turned(tiles[m])
        for j in range(SLOTS):
            piece = paired(matrix, j)
            pt[j, m * 128 : (m + 1) * 128, 0 : piece.shape[1]] = piece

    def chunk(buf, j):
        if j == 0:
            return buf[0, 0:ROWS]
        if j == 8:
            return buf[0, ROWS : 2 * ROWS]
        return buf[j]

    def multiply(i, k):
        total = []
        buf = buffer(k)

        def consume(b):
            left = pd[i, b, :, 0:ROWS] if b in (0, 8) else pd[i, b]
            right = rhs[0, 0] if (k == 0 and b == 0) else chunk(buf, b)
            term = dot(left, right)
            if total:
                total[0] = total[0] + term
            else:
                total.append(term)

        return total, consume

    sources = [source_s[0, 0, m] for m in range(TILES)]
    blocks = [block_s[0, 0, m] for m in range(TILES)]
    live = count_s[0, 0]

    def earlier(which):
        for m in range(TILES):
            rows = slice(m * 128, (m + 1) * 128)
            at = jnp.minimum(sources[m], CHAIN - 2)
            total = None if 0 in which else old[m]
            for b in which:
                left = pt[b, rows, 0:ROWS] if b in (0, 8) else pt[b, rows]
                if b == 0:
                    right = gx[at, 0, 0:ROWS]
                elif b == 8:
                    right = gx[at, 0, ROWS : 2 * ROWS]
                else:
                    right = gx[at, b]
                term = dot(left, right)
                total = term if total is None else total + term
            old[m] = total

    mine = lax.rem(y, 2) * SIDE + x
    columns = pl.ds(pl.multiple_of(mine * 128, 128), 128)

    def spread(src, dst, send, recv):
        return [
            pltpu.make_async_remote_copy(
                src_ref=src, dst_ref=dst.at[mine], send_sem=send.at[i], recv_sem=recv.at[mine],
                device_id={"leaf": other}, device_id_type=pl.DeviceIdType.MESH,
            )
            for i, other in enumerate(near)
        ]

    def arrive(src, dst, send, recv):
        for i, other in enumerate(near):
            pltpu.make_async_remote_copy(
                src_ref=src, dst_ref=dst.at[i], send_sem=send.at[i], recv_sem=recv.at[i],
                device_id={"leaf": other}, device_id_type=pl.DeviceIdType.MESH,
            ).wait_recv()

    def side_dots(i, which):
        total = None if 0 in which else tacc[...]
        for b in which:
            left = pd[i, b, :, 0:ROWS] if b in (0, 8) else pd[i, b]
            term = dot(left, chunk(gb, b))
            total = term if total is None else total + term
        tacc[...] = total

    t_args = (tacc, tfull, t_send, t_recv)
    w_args = (tacc, wfull, w_send, w_recv)

    def window_0a():
        prepare(0, 1)

    def window_0b():
        for load in loads[2:]:
            load.wait()
        gb[0, 0:ROWS] = jnp.where(core == 0, suba[0, :, columns], dinva[0, :, columns])
        send_own(9)
        prepare(2)

    def window_1a():
        pass_on(9, (1,))
        prepare(3, 4)

    def window_1b():
        pass_on(9, (2,))
        prepare(5)
        prepare_tile(0)

    def window_2a():
        pass_on(9, (3,))
        prepare(6)
        prepare_tile(1)

    def window_2b():
        pass_on(9, (4,))
        store_pairs(7, turned(dinva[1]))

    def window_3a():
        pass_on(9, (5,))
        prepare_tile(2)

    def window_3b():
        pass_on(9, (6,))

        @pl.when(core == 0)
        def _():
            side_dots(7, range(0, 6))

    def window_4a():
        pass_on(9, (7,))

        @pl.when(core == 0)
        def _():
            side_dots(7, range(6, 8))

    def window_4b():
        receive(9, 8)

        @pl.when(core == 0)
        def _():
            side_dots(7, range(8, 9))
            for copy in spread(*t_args):
                copy.start()

    def window_5b():
        @pl.when(core == 1)
        def _():
            arrive(*t_args)
            store_pairs(8, turned(jnp.concatenate([tfull[i] for i in range(8)], axis=1)))
            side_dots(8, range(0, 2))

    def window_6a():
        earlier(range(0, 3))

        @pl.when(core == 1)
        def _():
            side_dots(8, range(2, 5))

    def window_6b():
        earlier(range(3, 6))

        @pl.when(core == 1)
        def _():
            side_dots(8, range(5, 9))
            for copy in spread(*w_args):
                copy.start()

    def window_7a():
        earlier(range(6, 9))
        place_rhs()

    windows = [
        (window_0a, window_0b), (window_1a, window_1b), (window_2a, window_2b), (window_3a, window_3b),
        (window_4a, window_4b), (None, window_5b), (window_6a, window_6b),
    ]

    loads[0].wait()
    loads[1].wait()
    for s in range(CHAIN):
        k = 2 * s
        total, consume = multiply(k, k)
        gather(k, consume, *windows[k])
        solved = total[0]
        buffer(k + 1)[0, 0:ROWS] = solved
        out_local[0, s] = solved
        if s + 1 < CHAIN:
            total, consume = multiply(k + 1, k + 1)
            gather(k + 1, consume, *windows[k + 1])
            buffer(k + 2)[0, 0:ROWS] = rhs[0, s + 1] - total[0]

    half = lax.rem(me, 2)
    home = lax.div(me, 2)
    lane = lax.broadcasted_iota(jnp.int32, (8, 128), 1)
    sub_at = lax.broadcasted_iota(jnp.int32, (8, 128), 0)
    inside = jnp.logical_and(lax.div(lane, ROWS) == half, lax.div(sub_at, 4) == core)
    def place_rhs():
        for a in range(2):
            prow[0:4, 0:ROWS] = rhs_anc[a]
            quad = prow[0:8]
            wide = jnp.where(sub_at < 4, quad, pltpu.roll(quad, 4, axis=0))
            wide = jnp.where(lane < ROWS, wide, pltpu.roll(wide, ROWS, axis=1))
            give[a] = jnp.where(inside, wide, 0.0)

    last = []

    def consume_last(b):
        left = pt[b, :, 0:ROWS] if b in (0, 8) else pt[b]
        term = dot(left, chunk(gl, b))
        if last:
            last[0] = last[0] + term
        else:
            last.append(term)

    gather(7, consume_last, window_7a)
    for m in range(TILES):
        term = jnp.where(sources[m] == CHAIN - 1, last[0][m * 128 : (m + 1) * 128], old[m])
        term = jnp.where(m < live, term, 0.0)
        cells[m] = jnp.transpose(term).reshape(N, 8, 128)

    def build(role, out):
        for d in range(SIDE):
            for e in range(SIDE):
                xx = jnp.where(role == 0, lax.rem(x + d, SIDE), lax.rem(x + e, SIDE))
                yy = jnp.where(role == 0, lax.rem(y + e, SIDE), lax.rem(y + d, SIDE))
                cell = yy * SIDE + xx
                pieces = [cells[m, cell] for m in range(TILES)]
                for b in range(8):
                    value = jnp.zeros((8, 128), F32)
                    for m in range(TILES):
                        value = value - jnp.where(blocks[m] == role * 8 + b, pieces[m], 0.0)
                    if d == 0 and e == 0:
                        value = value + jnp.where(home == b, give[role], 0.0)
                    out[d, e, b] = value

    def remote(src, dst, send, recv, **where):
        return pltpu.make_async_remote_copy(
            src_ref=src, dst_ref=dst, send_sem=send, recv_sem=recv, device_id=where, device_id_type=pl.DeviceIdType.MESH
        )

    build(1 - core, theirs)
    pairs = [remote(theirs.at[d], pool.at[d], pair_send.at[d], pair_recv.at[d], leaf=partner) for d in range(SIDE)]
    for d in (2, 1, 3, 0):
        pairs[d].start()
    build(core, mid)
    ones = [None] + [
        remote(mid.at[d], inbox1.at[d - 1], one_send.at[d - 1], one_recv.at[d - 1], leaf=one_of[d]) for d in range(1, SIDE)
    ]
    for d in (2, 1, 3, 0):
        pairs[d].wait_recv()
        mid[d] = mid[d] + pool[d]
        if d:
            ones[d].start()
    for d in (1, 3, 2):
        ones[d].wait_recv()
    zbuf[...] = mid[0] + inbox1[0] + inbox1[1] + inbox1[2]
    twos = [None] + [
        remote(zbuf.at[d], inbox2.at[d - 1], two_send.at[d - 1], two_recv.at[d - 1], leaf=two_of[d]) for d in range(1, SIDE)
    ]
    for d in (2, 1, 3):
        twos[d].start()
    for d in (1, 3, 2):
        twos[d].wait_recv()
    gz[0, 0:ROWS] = (zbuf[0] + inbox2[0] + inbox2[1] + inbox2[2]).reshape(ROWS, RHS)

    sums = []

    def add_up(b):
        piece = chunk(gz, b)
        if b not in (0, 8):
            piece = piece[0:ROWS] + piece[ROWS : 2 * ROWS]
        if sums:
            sums[0] = sums[0] + piece
        else:
            sums.append(piece)

    gather(8, add_up)
    wanted = sums[0]
    first = jnp.zeros((8, ROWS), F32)
    for b in range(8):
        first = first + dot_nt(wanted[b * 8 : b * 8 + 8], dinva[core, :, b * 128 : (b + 1) * 128])

    def swap(src, dst, i):
        return remote(src, dst, swap_send.at[i], swap_recv.at[i], leaf=partner)

    def down():
        return swap(swap_out, swap_in, 0)

    def back():
        return swap(swap_out.at[1], swap_in.at[1], 1)

    @pl.when(core == 0)
    def _():
        arrive(*w_args)
        second = jnp.zeros((8, ROWS), F32)
        for b in range(8):
            second = second + dot_nt(wanted[b * 8 : b * 8 + 8], wfull[b])
        swap_out[0, :, 0:ROWS] = first
        swap_out[1, :, 0:ROWS] = second
        down().start()
        back().wait_recv()
        for a in range(2):
            out_anc[a] = (swap_out[0] if a == 0 else swap_in[1])[0:4, 0:ROWS]
        down().wait_send()
        for copy in spread(*t_args):
            copy.wait_send()

    @pl.when(core == 1)
    def _():
        down().wait_recv()
        swap_out[1, :, 0:ROWS] = first - swap_in[1, :, 0:ROWS]
        back().start()
        for a in range(2):
            out_anc[a] = (swap_in[0] if a == 0 else swap_out[1])[4:8, 0:ROWS]
        back().wait_send()
        for copy in spread(*w_args):
            copy.wait_send()

    for k in range(10):
        finish(k)
    for d in range(SIDE):
        pairs[d].wait_send()
        if d:
            ones[d].wait_send()
            twos[d].wait_send()


def on_device(rhs_local, diag_inv_local, sub_local, tiles, tile_block, tile_source, tile_count, rhs_anc, diag_inv_anc, sub_anc):
    vmem = pl.BlockSpec(memory_space=pltpu.VMEM)
    smem = pl.BlockSpec(memory_space=pltpu.SMEM)
    hbm = pl.BlockSpec(memory_space=pl.ANY)
    dma = pltpu.SemaphoreType.DMA
    local, anc = pl.pallas_call(
        kernel,
        out_shape=(
            jax.ShapeDtypeStruct((1, CHAIN, ROWS, RHS), F32),
            jax.ShapeDtypeStruct((2, 4, ROWS), F32),
        ),
        in_specs=[smem, smem, smem, vmem, vmem, hbm, hbm, hbm, hbm, hbm],
        out_specs=(vmem, vmem),
        scratch_shapes=[
            pltpu.VMEM((4, ROWS, 1024), F32),
            pltpu.VMEM((3, ROWS, 1024), F32),
            pltpu.VMEM((TILES, 128, 1024), F32),
            pltpu.VMEM((2, ROWS, 1024), F32),
            pltpu.VMEM((1, ROWS, 1024), F32),
            pltpu.VMEM((9, SLOTS, ROWS, 128), F32),
            pltpu.VMEM((SLOTS, TILES * 128, 128), F32),
            pltpu.VMEM((4, 8, 128, RHS), F32),
            pltpu.VMEM((3, 8, 128, RHS), F32),
            pltpu.VMEM((8, 128, RHS), F32),
            pltpu.VMEM((8, 128, RHS), F32),
            pltpu.VMEM((TILES, 128, RHS), F32),
            pltpu.VMEM((TILES, N, 8, 128), F32),
            pltpu.VMEM((SIDE, SIDE, 8, 8, 128), F32),
            pltpu.VMEM((SIDE, SIDE, 8, 8, 128), F32),
            pltpu.VMEM((3, SIDE, 8, 8, 128), F32),
            pltpu.VMEM((SIDE, SIDE, 8, 8, 128), F32),
            pltpu.VMEM((3, 8, 8, 128), F32),
            pltpu.VMEM((SIDE, 8, 8, 128), F32),
            pltpu.VMEM((8, 128, RHS), F32),
            pltpu.VMEM((ROWS, 128), F32),
            pltpu.VMEM((8, ROWS, 128), F32),
            pltpu.VMEM((8, ROWS, 128), F32),
            pltpu.VMEM((2, 8, 128), F32),
            pltpu.VMEM((2, 8, 128), F32),
            pltpu.VMEM((2, 8, 128), F32),
            pltpu.VMEM((8, 128), F32),
            dma((5,)),
            dma((10, 2, 8, PIECES)),
            dma((10, 2, 8, PIECES)),
            dma((SIDE,)),
            dma((SIDE,)),
            dma((3,)),
            dma((3,)),
            dma((3,)),
            dma((3,)),
            dma((8,)),
            dma((8,)),
            dma((8,)),
            dma((8,)),
            dma((2,)),
            dma((2,)),
        ],
        compiler_params=pltpu.CompilerParams(
            collective_id=0, has_side_effects=True, vmem_limit_bytes=56 * 1024 * 1024
        ),
    )(tile_block, tile_source, tile_count, rhs_local, jnp.transpose(rhs_anc, (0, 2, 1)), diag_inv_local, sub_local, tiles, diag_inv_anc, sub_anc)
    return local, jnp.transpose(anc, (0, 2, 1))


def solution(mesh):
    return jax.shard_map(
        on_device,
        mesh=mesh,
        in_specs=(
            P("leaf", None, "grp", None),
            P("leaf", None, "grp", None),
            P("leaf", None, "grp", None),
            P("leaf", "grp", None, None, None),
            P("leaf", "grp", None),
            P("leaf", "grp", None),
            P("leaf", "grp"),
            P(None, "grp", "leaf"),
            P(None, "grp", None),
            P(None, "grp", None),
        ),
        out_specs=(P("leaf", None, "grp", None), P(None, "grp", "leaf")),
        check_vma=False,
    )
```

```python
import jax
import jax.numpy as jnp
from jax import lax
from jax.experimental import pallas as pl
from jax.experimental.pallas import tpu as pltpu
from jax.sharding import PartitionSpec as P

HI = lax.Precision.HIGHEST
F32 = jnp.float32
N = 16
SIDE = 4
CHAIN = 4
ROWS = 64
RHS = 128
TILES = 3
SLOTS = 9

CHILDREN = {0: (5, 1), 1: (2,), 2: (3,), 5: (8, 7, 6, 4)}
RELAYS = ((1,), (5,), (2,))
EARLY = (1,)
LATE = (6, 4, 3, 7, 8)
RING = {i: (i + 1,) for i in range(8)}
PIECES = 2
EDGES = sorted({abs(b - a) for tree in (CHILDREN, RING) for a, bs in tree.items() for b in bs})


def dot(a, b):
    return jnp.dot(a, b, precision=HI, preferred_element_type=F32)


def dot_nt(a, b):
    return lax.dot_general(a, b, (((1,), (1,)), ((), ())), precision=HI, preferred_element_type=F32)


def kernel(
    block_s, source_s, count_s, rhs, rhs_anc, dinv_h, sub_h, tiles_h, dinva_h, suba_h,
    out_local, out_anc,
    dinv, sub, tiles, dinva, suba,
    pd, pt, gr, gx, gl, gz, old, cells, pool, theirs, inbox1, mid, inbox2, zbuf, gb, tacc, tfull, wfull, give, swap_out, swap_in, prow,
    load_sem, send_sem, recv_sem, pair_send, pair_recv, one_send, one_recv, two_send, two_recv,
    t_send, t_recv, w_send, w_recv, swap_send, swap_recv,
):
    me = lax.axis_index("grp")
    leaf = lax.axis_index("leaf")
    core = lax.rem(leaf, 2)
    x = lax.rem(lax.div(leaf, 2), SIDE)
    y = lax.div(leaf, 2 * SIDE)
    partner = leaf + 1 - 2 * core
    p_one = jnp.where(core == 0, x, y)
    p_two = jnp.where(core == 0, y, x)

    def leaf_of(one, two):
        xx = jnp.where(core == 0, one, two)
        yy = jnp.where(core == 0, two, one)
        return (yy * SIDE + xx) * 2 + core

    def z_at(step):
        return lax.rem(me + (step + 2 * N), N)

    one_of = [leaf_of(lax.rem(p_one + d, SIDE), p_two) for d in range(SIDE)]
    two_of = [leaf_of(p_one, lax.rem(p_two + d, SIDE)) for d in range(SIDE)]

    loads = [
        pltpu.make_async_copy(src, dst, load_sem.at[i])
        for i, (src, dst) in enumerate(
            ((dinv_h.at[0], dinv), (sub_h.at[0], sub), (tiles_h.at[0, 0], tiles), (dinva_h, dinva), (suba_h, suba))
        )
    ]
    for load in loads:
        load.start()

    prow[...] = jnp.zeros_like(prow)
    swap_out[...] = jnp.zeros_like(swap_out)
    barrier = pltpu.get_barrier_semaphore()
    greeted = 0
    for step in EDGES:
        for sign in (1, -1):
            pl.semaphore_signal(barrier, inc=1, device_id={"grp": z_at(sign * step)}, device_id_type=pl.DeviceIdType.MESH)
            greeted += 1
    near = [((lax.div(y, 2) * 2 + dy) * SIDE + dx) * 2 + 1 - core for dy in range(2) for dx in range(SIDE)]
    for other in (*near, *one_of[1:], *two_of[1:]):
        pl.semaphore_signal(barrier, inc=1, device_id={"leaf": other}, device_id_type=pl.DeviceIdType.MESH)
        greeted += 1
    pl.semaphore_wait(barrier, greeted)

    def buffer(k):
        if k == 9:
            return gb
        if k == 8:
            return gz
        if k == 7:
            return gl
        return gr.at[k // 2] if k % 2 == 0 else gx.at[k // 2]

    part = ROWS // PIECES

    def view(k, d, b, p):
        buf = buffer(k)
        if b == 0:
            return rhs.at[0, 0, p * part : (p + 1) * part] if k == 0 else buf.at[0, p * part : (p + 1) * part]
        base = ROWS if b == 8 else ROWS * d
        return buf.at[b % 8, base + p * part : base + (p + 1) * part]

    def ways(b, p):
        return (0, 1) if b < 8 else (2 * p // PIECES,)

    def edge(k, d, a, b, p):
        step = b - a if d == 0 else a - b
        return pltpu.make_async_remote_copy(
            src_ref=view(k, d, a, p),
            dst_ref=view(k, d, b, p),
            send_sem=send_sem.at[k, d, b - 1, p],
            recv_sem=recv_sem.at[k, d, b - 1, p],
            device_id={"grp": z_at(step)},
            device_id_type=pl.DeviceIdType.MESH,
        )

    def tree(k):
        return RING if k == 9 else CHILDREN

    parents = {k: {b: a for a, bs in tree(k).items() for b in bs} for k in range(10)}

    def send_own(k):
        for b in tree(k)[0]:
            for p in range(PIECES):
                for d in ways(b, p):
                    edge(k, d, 0, b, p).start()

    def receive(k, b):
        for p in range(PIECES):
            for d in ways(b, p):
                edge(k, d, parents[k][b], b, p).wait_recv()

    def pass_on(k, relays):
        for p in range(PIECES):
            for b in relays:
                for d in ways(b, p):
                    edge(k, d, parents[k][b], b, p).wait_recv()
                for c in tree(k)[b]:
                    for d in ways(c, p):
                        edge(k, d, b, c, p).start()

    def gather(k, consume, first=None, second=None):
        send_own(k)
        if first is not None:
            first()
        consume(0)
        relays = [b for phase in RELAYS for b in phase]
        pass_on(k, RELAYS[0])
        for b in EARLY:
            if b not in relays:
                receive(k, b)
            consume(b)
        for phase in RELAYS[1:]:
            pass_on(k, phase)
            for b in phase:
                consume(b)
        if second is not None:
            second()
        for b in LATE:
            receive(k, b)
            consume(b)

    def finish(k):
        for b, a in parents[k].items():
            for p in range(PIECES):
                for d in ways(b, p):
                    edge(k, d, a, b, p).wait_send()

    shift = lax.rem((N - me) * ROWS, N * ROWS)

    def turned(matrix):
        return pltpu.roll(matrix, shift, axis=1)

    def paired(matrix, j):
        if j == 0:
            return matrix[:, 0:ROWS]
        if j == 8:
            return matrix[:, 8 * ROWS : 9 * ROWS]
        return jnp.concatenate(
            [matrix[:, (N - j) * ROWS : (N - j + 1) * ROWS], matrix[:, j * ROWS : (j + 1) * ROWS]], axis=1
        )

    def store_pairs(i, matrix):
        for j in range(SLOTS):
            piece = paired(matrix, j)
            pd[i, j, :, 0 : piece.shape[1]] = piece

    def prepare(*which):
        for i in which:
            store_pairs(i, turned(dinv[i // 2] if i % 2 == 0 else sub[i // 2]))

    def prepare_tile(m):
        matrix = turned(tiles[m])
        for j in range(SLOTS):
            piece = paired(matrix, j)
            pt[j, m * 128 : (m + 1) * 128, 0 : piece.shape[1]] = piece

    def chunk(buf, j):
        if j == 0:
            return buf[0, 0:ROWS]
        if j == 8:
            return buf[0, ROWS : 2 * ROWS]
        return buf[j]

    def multiply(i, k):
        total = []
        buf = buffer(k)

        def consume(b):
            left = pd[i, b, :, 0:ROWS] if b in (0, 8) else pd[i, b]
            right = rhs[0, 0] if (k == 0 and b == 0) else chunk(buf, b)
            term = dot(left, right)
            if total:
                total[0] = total[0] + term
            else:
                total.append(term)

        return total, consume

    sources = [source_s[0, 0, m] for m in range(TILES)]
    blocks = [block_s[0, 0, m] for m in range(TILES)]
    live = count_s[0, 0]

    def earlier(which):
        for m in range(TILES):
            rows = slice(m * 128, (m + 1) * 128)
            at = jnp.minimum(sources[m], CHAIN - 2)
            total = None if 0 in which else old[m]
            for b in which:
                left = pt[b, rows, 0:ROWS] if b in (0, 8) else pt[b, rows]
                if b == 0:
                    right = gx[at, 0, 0:ROWS]
                elif b == 8:
                    right = gx[at, 0, ROWS : 2 * ROWS]
                else:
                    right = gx[at, b]
                term = dot(left, right)
                total = term if total is None else total + term
            old[m] = total

    mine = lax.rem(y, 2) * SIDE + x
    columns = pl.ds(pl.multiple_of(mine * 128, 128), 128)

    def spread(src, dst, send, recv):
        return [
            pltpu.make_async_remote_copy(
                src_ref=src, dst_ref=dst.at[mine], send_sem=send.at[i], recv_sem=recv.at[mine],
                device_id={"leaf": other}, device_id_type=pl.DeviceIdType.MESH,
            )
            for i, other in enumerate(near)
        ]

    def arrive(src, dst, send, recv):
        for i, other in enumerate(near):
            pltpu.make_async_remote_copy(
                src_ref=src, dst_ref=dst.at[i], send_sem=send.at[i], recv_sem=recv.at[i],
                device_id={"leaf": other}, device_id_type=pl.DeviceIdType.MESH,
            ).wait_recv()

    def side_dots(i, which):
        total = None if 0 in which else tacc[...]
        for b in which:
            left = pd[i, b, :, 0:ROWS] if b in (0, 8) else pd[i, b]
            term = dot(left, chunk(gb, b))
            total = term if total is None else total + term
        tacc[...] = total

    t_args = (tacc, tfull, t_send, t_recv)
    w_args = (tacc, wfull, w_send, w_recv)

    def window_0a():
        prepare(0, 1)

    def window_0b():
        for load in loads[2:]:
            load.wait()
        gb[0, 0:ROWS] = jnp.where(core == 0, suba[0, :, columns], dinva[0, :, columns])
        send_own(9)
        prepare(2)

    def window_1a():
        pass_on(9, (1,))
        prepare(3, 4)

    def window_1b():
        pass_on(9, (2,))
        prepare(5)
        prepare_tile(0)

    def window_2a():
        pass_on(9, (3,))
        prepare(6)
        prepare_tile(1)

    def window_2b():
        pass_on(9, (4,))
        store_pairs(7, turned(dinva[1]))

    def window_3a():
        pass_on(9, (5,))
        prepare_tile(2)

    def window_3b():
        pass_on(9, (6,))

        @pl.when(core == 0)
        def _():
            side_dots(7, range(0, 6))

    def window_4a():
        pass_on(9, (7,))

        @pl.when(core == 0)
        def _():
            side_dots(7, range(6, 8))

    def window_4b():
        receive(9, 8)

        @pl.when(core == 0)
        def _():
            side_dots(7, range(8, 9))
            for copy in spread(*t_args):
                copy.start()

    def window_5b():
        @pl.when(core == 1)
        def _():
            arrive(*t_args)
            store_pairs(8, turned(jnp.concatenate([tfull[i] for i in range(8)], axis=1)))
            side_dots(8, range(0, 2))

    def window_6a():
        earlier(range(0, 3))

        @pl.when(core == 1)
        def _():
            side_dots(8, range(2, 5))

    def window_6b():
        earlier(range(3, 6))

        @pl.when(core == 1)
        def _():
            side_dots(8, range(5, 9))
            for copy in spread(*w_args):
                copy.start()

    def window_7a():
        earlier(range(6, 9))
        place_rhs()

    windows = [
        (window_0a, window_0b), (window_1a, window_1b), (window_2a, window_2b), (window_3a, window_3b),
        (window_4a, window_4b), (None, window_5b), (window_6a, window_6b),
    ]

    loads[0].wait()
    loads[1].wait()
    for s in range(CHAIN):
        k = 2 * s
        total, consume = multiply(k, k)
        gather(k, consume, *windows[k])
        solved = total[0]
        buffer(k + 1)[0, 0:ROWS] = solved
        out_local[0, s] = solved
        if s + 1 < CHAIN:
            total, consume = multiply(k + 1, k + 1)
            gather(k + 1, consume, *windows[k + 1])
            buffer(k + 2)[0, 0:ROWS] = rhs[0, s + 1] - total[0]

    half = lax.rem(me, 2)
    home = lax.div(me, 2)
    lane = lax.broadcasted_iota(jnp.int32, (8, 128), 1)
    sub_at = lax.broadcasted_iota(jnp.int32, (8, 128), 0)
    inside = jnp.logical_and(lax.div(lane, ROWS) == half, lax.div(sub_at, 4) == core)
    def place_rhs():
        for a in range(2):
            prow[0:4, 0:ROWS] = rhs_anc[a]
            quad = prow[0:8]
            wide = jnp.where(sub_at < 4, quad, pltpu.roll(quad, 4, axis=0))
            wide = jnp.where(lane < ROWS, wide, pltpu.roll(wide, ROWS, axis=1))
            give[a] = jnp.where(inside, wide, 0.0)

    last = []

    def consume_last(b):
        left = pt[b, :, 0:ROWS] if b in (0, 8) else pt[b]
        term = dot(left, chunk(gl, b))
        if last:
            last[0] = last[0] + term
        else:
            last.append(term)

    gather(7, consume_last, window_7a)
    for m in range(TILES):
        term = jnp.where(sources[m] == CHAIN - 1, last[0][m * 128 : (m + 1) * 128], old[m])
        term = jnp.where(m < live, term, 0.0)
        cells[m] = jnp.transpose(term).reshape(N, 8, 128)

    def build(role, out):
        for d in range(SIDE):
            for e in range(SIDE):
                xx = jnp.where(role == 0, lax.rem(x + d, SIDE), lax.rem(x + e, SIDE))
                yy = jnp.where(role == 0, lax.rem(y + e, SIDE), lax.rem(y + d, SIDE))
                cell = yy * SIDE + xx
                pieces = [cells[m, cell] for m in range(TILES)]
                for b in range(8):
                    value = jnp.zeros((8, 128), F32)
                    for m in range(TILES):
                        value = value - jnp.where(blocks[m] == role * 8 + b, pieces[m], 0.0)
                    if d == 0 and e == 0:
                        value = value + jnp.where(home == b, give[role], 0.0)
                    out[d, e, b] = value

    def remote(src, dst, send, recv, **where):
        return pltpu.make_async_remote_copy(
            src_ref=src, dst_ref=dst, send_sem=send, recv_sem=recv, device_id=where, device_id_type=pl.DeviceIdType.MESH
        )

    build(1 - core, theirs)
    pairs = [remote(theirs.at[d], pool.at[d], pair_send.at[d], pair_recv.at[d], leaf=partner) for d in range(SIDE)]
    for d in (2, 1, 3, 0):
        pairs[d].start()
    build(core, mid)
    ones = [None] + [
        remote(mid.at[d], inbox1.at[d - 1], one_send.at[d - 1], one_recv.at[d - 1], leaf=one_of[d]) for d in range(1, SIDE)
    ]
    for d in (2, 1, 3, 0):
        pairs[d].wait_recv()
        mid[d] = mid[d] + pool[d]
        if d:
            ones[d].start()
    for d in (1, 3, 2):
        ones[d].wait_recv()
    zbuf[...] = mid[0] + inbox1[0] + inbox1[1] + inbox1[2]
    twos = [None] + [
        remote(zbuf.at[d], inbox2.at[d - 1], two_send.at[d - 1], two_recv.at[d - 1], leaf=two_of[d]) for d in range(1, SIDE)
    ]
    for d in (2, 1, 3):
        twos[d].start()
    for d in (1, 3, 2):
        twos[d].wait_recv()
    gz[0, 0:ROWS] = (zbuf[0] + inbox2[0] + inbox2[1] + inbox2[2]).reshape(ROWS, RHS)

    sums = []

    def add_up(b):
        piece = chunk(gz, b)
        if b not in (0, 8):
            piece = piece[0:ROWS] + piece[ROWS : 2 * ROWS]
        if sums:
            sums[0] = sums[0] + piece
        else:
            sums.append(piece)

    gather(8, add_up)
    wanted = sums[0]
    first = jnp.zeros((8, ROWS), F32)
    for b in range(8):
        first = first + dot_nt(wanted[b * 8 : b * 8 + 8], dinva[core, :, b * 128 : (b + 1) * 128])

    def swap(src, dst, i):
        return remote(src, dst, swap_send.at[i], swap_recv.at[i], leaf=partner)

    def down():
        return swap(swap_out, swap_in, 0)

    def back():
        return swap(swap_out.at[1], swap_in.at[1], 1)

    @pl.when(core == 0)
    def _():
        arrive(*w_args)
        second = jnp.zeros((8, ROWS), F32)
        for b in range(8):
            second = second + dot_nt(wanted[b * 8 : b * 8 + 8], wfull[b])
        swap_out[0, :, 0:ROWS] = first
        swap_out[1, :, 0:ROWS] = second
        down().start()
        back().wait_recv()
        for a in range(2):
            out_anc[a] = (swap_out[0] if a == 0 else swap_in[1])[0:4, 0:ROWS]
        down().wait_send()
        for copy in spread(*t_args):
            copy.wait_send()

    @pl.when(core == 1)
    def _():
        down().wait_recv()
        swap_out[1, :, 0:ROWS] = first - swap_in[1, :, 0:ROWS]
        back().start()
        for a in range(2):
            out_anc[a] = (swap_in[0] if a == 0 else swap_out[1])[4:8, 0:ROWS]
        back().wait_send()
        for copy in spread(*w_args):
            copy.wait_send()

    for k in range(10):
        finish(k)
    for d in range(SIDE):
        pairs[d].wait_send()
        if d:
            ones[d].wait_send()
            twos[d].wait_send()


def on_device(rhs_local, diag_inv_local, sub_local, tiles, tile_block, tile_source, tile_count, rhs_anc, diag_inv_anc, sub_anc):
    vmem = pl.BlockSpec(memory_space=pltpu.VMEM)
    smem = pl.BlockSpec(memory_space=pltpu.SMEM)
    hbm = pl.BlockSpec(memory_space=pl.ANY)
    dma = pltpu.SemaphoreType.DMA
    local, anc = pl.pallas_call(
        kernel,
        out_shape=(
            jax.ShapeDtypeStruct((1, CHAIN, ROWS, RHS), F32),
            jax.ShapeDtypeStruct((2, 4, ROWS), F32),
        ),
        in_specs=[smem, smem, smem, vmem, vmem, hbm, hbm, hbm, hbm, hbm],
        out_specs=(vmem, vmem),
        scratch_shapes=[
            pltpu.VMEM((4, ROWS, 1024), F32),
            pltpu.VMEM((3, ROWS, 1024), F32),
            pltpu.VMEM((TILES, 128, 1024), F32),
            pltpu.VMEM((2, ROWS, 1024), F32),
            pltpu.VMEM((1, ROWS, 1024), F32),
            pltpu.VMEM((9, SLOTS, ROWS, 128), F32),
            pltpu.VMEM((SLOTS, TILES * 128, 128), F32),
            pltpu.VMEM((4, 8, 128, RHS), F32),
            pltpu.VMEM((3, 8, 128, RHS), F32),
            pltpu.VMEM((8, 128, RHS), F32),
            pltpu.VMEM((8, 128, RHS), F32),
            pltpu.VMEM((TILES, 128, RHS), F32),
            pltpu.VMEM((TILES, N, 8, 128), F32),
            pltpu.VMEM((SIDE, SIDE, 8, 8, 128), F32),
            pltpu.VMEM((SIDE, SIDE, 8, 8, 128), F32),
            pltpu.VMEM((3, SIDE, 8, 8, 128), F32),
            pltpu.VMEM((SIDE, SIDE, 8, 8, 128), F32),
            pltpu.VMEM((3, 8, 8, 128), F32),
            pltpu.VMEM((SIDE, 8, 8, 128), F32),
            pltpu.VMEM((8, 128, RHS), F32),
            pltpu.VMEM((ROWS, 128), F32),
            pltpu.VMEM((8, ROWS, 128), F32),
            pltpu.VMEM((8, ROWS, 128), F32),
            pltpu.VMEM((2, 8, 128), F32),
            pltpu.VMEM((2, 8, 128), F32),
            pltpu.VMEM((2, 8, 128), F32),
            pltpu.VMEM((8, 128), F32),
            dma((5,)),
            dma((10, 2, 8, PIECES)),
            dma((10, 2, 8, PIECES)),
            dma((SIDE,)),
            dma((SIDE,)),
            dma((3,)),
            dma((3,)),
            dma((3,)),
            dma((3,)),
            dma((8,)),
            dma((8,)),
            dma((8,)),
            dma((8,)),
            dma((2,)),
            dma((2,)),
        ],
        compiler_params=pltpu.CompilerParams(
            collective_id=0, has_side_effects=True, vmem_limit_bytes=56 * 1024 * 1024
        ),
    )(tile_block, tile_source, tile_count, rhs_local, jnp.transpose(rhs_anc, (0, 2, 1)), diag_inv_local, sub_local, tiles, diag_inv_anc, sub_anc)
    return local, jnp.transpose(anc, (0, 2, 1))


def solution(mesh):
    return jax.shard_map(
        on_device,
        mesh=mesh,
        in_specs=(
            P("leaf", None, "grp", None),
            P("leaf", None, "grp", None),
            P("leaf", None, "grp", None),
            P("leaf", "grp", None, None, None),
            P("leaf", "grp", None),
            P("leaf", "grp", None),
            P("leaf", "grp"),
            P(None, "grp", "leaf"),
            P(None, "grp", None),
            P(None, "grp", None),
        ),
        out_specs=(P("leaf", None, "grp", None), P(None, "grp", "leaf")),
        check_vma=False,
    )
```
